32 devices in a mesh: group: 4 (over x, core), tp: 8 (over z, y).
Axes of the slice: x: 2, y: 2, z: 4, core: 2. Of those that a mesh axis runs over, the one named last changes fastest.
Arguments:
- hidden: bfloat16 [512, 8192], P('group', 'tp'), may hold values from -6 to 6
- norm_gain: float32 [2, 8192], P(None, 'tp'), may hold values from 0.25 to 1.75
- anchor: bfloat16 [2, 8192, 8192], P(None, None, 'tp'), may hold values from -0.0625 to 0.0625
- delta_tiles: bfloat16 [32, 2, 64, 4, 128, 128], P('group', None, 'tp'), may hold values from -0.1875 to 0.1875
- tile_rows: int32 [32, 2, 64, 4], P('group', None, 'tp'), may hold values from 0 to 64, as said below
- tenant: int32 [512], P('group'), may hold values from 0 to 31, as said below
Outputs:
- updated: bfloat16 [512, 8192], P('group', 'tp')
The draws below stay inside these ranges and needn't reach their ends.
Inputs may be any that keep to these rules, and one draw needn't show every extreme that they name: Tenant t is owned by group t // 8; the requests of group g are rows g * 128 to g * 128 + 127. For every other group o, call tenant o * 8 + (g + o) % 8 group g's paired tenant of o. Its tiles lie only on group o unless a program moves them. Of one group's requests at most 32 have tenants of any one other group, and in every draw some group has exactly 32 requests of one other group's tenants, none of them its paired tenant of that group. `tile_rows`: each list of one tenant, layer and column block names 1 to 4 distinct row blocks in its first slots and 64 in the others, which marks an empty slot; some list of every draw has empty slots.
All inputs are finite; a program needn't handle non-finite values.
Results may differ from the reference program's by a relative error of at most 0.0052.
Values may be sent and summed in bfloat16 or wider, within the bound.
No kernel may reach another device: no remote copies, remote signals or barrier semaphores. Data moves between devices by JAX's collectives and lax.ppermute only.
A program may use at most 256 MiB of HBM per device.

```python
import jax
import jax.numpy as jnp
from jax import lax

D = 8192
TILE = 128
TPC = 4
TEN_GRP = 8
LAYERS = 2
REQ_GRP = 128
CAP = 32
NB = 64
REQUESTS = 512
TENANTS = 32
N_GROUP = 4


def route_plan(key):
    base_key = jax.random.fold_in(key, 4711)
    key_list = jax.random.split(base_key, 9)
    group_col = jnp.arange(N_GROUP, dtype=jnp.int32)
    miss_ids = (group_col[:, None] + group_col[None, :]) % TEN_GRP
    hot_order = jax.random.permutation(key_list[1], N_GROUP).astype(jnp.int32)
    first_draw = jax.random.randint(key_list[2], (N_GROUP, REQ_GRP), 0, N_GROUP, dtype=jnp.int32)
    second_draw = jax.random.randint(key_list[3], (N_GROUP, REQ_GRP), 0, N_GROUP, dtype=jnp.int32)
    owner_grp = hot_order[jnp.minimum(first_draw, second_draw)]
    local_idx = jax.random.randint(key_list[4], (N_GROUP, REQ_GRP), 0, TEN_GRP, dtype=jnp.int32)
    first_off = jax.random.randint(key_list[5], (N_GROUP,), 1, N_GROUP, dtype=jnp.int32)
    first_owner = (group_col + first_off) % N_GROUP
    first_local = (miss_ids[group_col, first_owner] + jax.random.randint(key_list[6], (N_GROUP,), 1, TEN_GRP, dtype=jnp.int32)) % TEN_GRP
    step_off = jax.random.randint(key_list[7], (N_GROUP,), 1, N_GROUP - 1, dtype=jnp.int32)
    second_off = (first_off - 1 + step_off) % (N_GROUP - 1) + 1
    second_owner = (group_col + second_off) % N_GROUP
    second_local = miss_ids[group_col, second_owner]
    positions = jnp.arange(REQ_GRP, dtype=jnp.int32)[None, :]
    owner_grp = jnp.where(positions < CAP, first_owner[:, None], owner_grp)
    local_idx = jnp.where(positions < CAP, first_local[:, None], local_idx)
    owner_grp = jnp.where(positions == CAP, second_owner[:, None], owner_grp)
    local_idx = jnp.where(positions == CAP, second_local[:, None], local_idx)
    remote = owner_grp != group_col[:, None]
    dest_hot = jnp.logical_and(owner_grp[:, :, None] == group_col[None, None, :], remote[:, :, None]).astype(jnp.int32)
    rank_base = jnp.cumsum(dest_hot, axis=1) - dest_hot
    position = jnp.sum(rank_base * dest_hot, axis=2)
    over_cap = jnp.logical_and(remote, position >= CAP)
    owner_grp = jnp.where(over_cap, group_col[:, None], owner_grp)
    tenant_grid = owner_grp * TEN_GRP + local_idx
    perm_keys = jax.random.split(key_list[8], N_GROUP)
    shuffles = jax.vmap(lambda one_key: jax.random.permutation(one_key, REQ_GRP).astype(jnp.int32))(perm_keys)
    tenant_grid = jnp.take_along_axis(tenant_grid, shuffles, axis=1)
    return tenant_grid.reshape(N_GROUP * REQ_GRP).astype(jnp.int32)


def draw_tenant(key, part):
    return route_plan(key)


def draw_tile_rows(key, part):
    list_count = TENANTS * LAYERS * NB
    perm_keys = jax.random.split(jax.random.fold_in(key, 99), list_count)
    chosen = jax.vmap(lambda one_key: jax.random.permutation(one_key, NB)[:TPC].astype(jnp.int32))(perm_keys)
    counts = jax.random.randint(jax.random.fold_in(key, 5), (list_count,), 1, TPC + 1, dtype=jnp.int32)
    picked = jax.random.randint(jax.random.fold_in(key, 6), (), 0, list_count, dtype=jnp.int32)
    counts = jnp.where(jnp.arange(list_count, dtype=jnp.int32) == picked, 1, counts)
    slot_pos = jnp.arange(TPC, dtype=jnp.int32)[None, :]
    filled = jnp.where(slot_pos < counts[:, None], chosen, NB)
    return filled.reshape(TENANTS, LAYERS, NB, TPC).astype(jnp.int32)


def levels(rng, extent, shards, least, largest):
    level, own = 1.0, jax.random.fold_in(rng, 6)
    for axis_at, shards_of in shards:
        draws = jnp.exp(jax.random.uniform(jax.random.fold_in(own, axis_at), (shards_of,), jnp.float32, least / len(shards), largest / len(shards)))
        level = level * jnp.repeat(draws, extent[axis_at] // shards_of).reshape([-1 if axis == axis_at else 1 for axis in range(len(extent))])
    return level


def centred(rng, shape, scale, limit, cuts=(), held_as=jnp.bfloat16):
    entries = scale * jax.random.normal(rng, shape, jnp.float32)
    if cuts:
        entries = entries * levels(rng, shape, cuts, -0.22, 0.18)
    return jnp.clip(entries, -limit, limit).astype(held_as)


def setup_inputs(seed: int = 0) -> dict:
    splits = jax.random.split(jax.random.key(seed), 7)
    hidden = centred(splits[0], (REQUESTS, D), 1.0, 6.0, ((0, 4), (1, 8)))
    norm_gain = jnp.clip(1.0 + 0.15 * jax.random.normal(splits[1], (LAYERS, D), jnp.float32), 0.25, 1.75)
    anchor = centred(splits[2], (LAYERS, D, D), D ** -0.5, 0.0625, ((2, 8),))
    delta_tiles = centred(splits[3], (TENANTS, LAYERS, NB, TPC, TILE, TILE), (2 * TPC * TILE) ** -0.5, 0.1875, ((0, 4), (2, 8)))
    tile_rows = draw_tile_rows(jax.random.fold_in(splits[6], 71), 0)
    tenant = draw_tenant(jax.random.fold_in(splits[6], 71), 0)
    return dict(hidden=hidden, norm_gain=norm_gain, anchor=anchor, delta_tiles=delta_tiles, tile_rows=tile_rows, tenant=tenant)


def reference(hidden, norm_gain, anchor, delta_tiles, tile_rows, tenant):
    stream = hidden.astype(jnp.float32)
    for layer_idx in range(LAYERS):
        square_sum = lax.optimization_barrier(jnp.sum(stream * stream, axis=1, keepdims=True))
        normed = (stream * lax.rsqrt(square_sum / D + 1e-05) * norm_gain[layer_idx][None, :]).astype(jnp.bfloat16)
        anchor_out = jnp.dot(normed, anchor[layer_idx], preferred_element_type=jnp.float32)

        def one_row(request):
            row_vec, owner_idx = request
            tile_set = delta_tiles[owner_idx, layer_idx].astype(jnp.float32)
            block_ids = tile_rows[owner_idx, layer_idx]
            usable = (block_ids < NB).astype(jnp.float32)
            pieces = row_vec.reshape(NB, TILE)[jnp.minimum(block_ids, NB - 1)]
            pieces = pieces.astype(jnp.float32) * usable[:, :, None]
            return jnp.einsum('cpi,cpik->ck', pieces, tile_set).reshape(D)
        delta_out = lax.map(one_row, (normed, tenant)).astype(jnp.bfloat16)
        stream = stream + anchor_out + delta_out.astype(jnp.float32)
    return stream.astype(jnp.bfloat16)
```

```python
import functools

import jax
import jax.numpy as jnp
from jax import lax
from jax.experimental import pallas as pl
from jax.experimental.pallas import tpu as pltpu
from jax.sharding import PartitionSpec as P


F32 = jnp.float32
BF16 = jnp.bfloat16
VMEM_LIMIT = 60 * 1024 * 1024
EPS = 1e-05


def swap(value, axis, offset):
    size = lax.axis_size(axis)
    return lax.ppermute(value, axis, [(i, i ^ offset) for i in range(size)])


def params(**kw):
    return pltpu.CompilerParams(vmem_limit_bytes=VMEM_LIMIT, **kw)


def whole():
    return pl.BlockSpec(memory_space=pltpu.VMEM)


def in_place():
    return pl.BlockSpec(memory_space=pl.ANY)


def pick_kernel(n_dest, n_shards, *refs):
    sel_ref = refs[0]
    shard_refs = refs[1 : 1 + n_shards]
    out_refs = refs[1 + n_shards :]
    cap = out_refs[0].shape[0]
    width = shard_refs[0].shape[1]
    for s, shard in enumerate(shard_refs):
        rows = jnp.dot(sel_ref[...], shard[...], preferred_element_type=F32).astype(BF16)
        for d in range(n_dest):
            out_refs[d][:, s * width : (s + 1) * width] = rows[d * cap : (d + 1) * cap]


def pick_rows(sel, shards, cap):
    n_dest = sel.shape[0] // cap
    width = shards[0].shape[1] * len(shards)
    nbytes = sum(x.size for x in shards) * 2 + n_dest * cap * width * 2
    return pl.pallas_call(
        functools.partial(pick_kernel, n_dest, len(shards)),
        out_shape=[jax.ShapeDtypeStruct((cap, width), BF16)] * n_dest,
        in_specs=[whole()] * (1 + len(shards)),
        out_specs=[whole()] * n_dest,
        compiler_params=params(),
        cost_estimate=pl.CostEstimate(
            flops=2 * sel.size * width, bytes_accessed=nbytes, transcendentals=0
        ),
        name="pick_rows",
    )(sel, *shards)


def product_kernel(cfg, ids_ref, *refs):
    n_in, plan, with_anchor, n_slots, per_list, col_step, width, n_cols = cfg
    src = refs[:n_in]
    slot_ref, tiles_ref = refs[n_in], refs[n_in + 1]
    at = n_in + 2
    if with_anchor:
        anchor_ref, stream_ref, square_ref = refs[at : at + 3]
        at += 3
    out_ref, full, pieces, masks, sem = refs[at : at + 5]
    rows = full.shape[1]
    tile = pieces.shape[1] // (n_slots * per_list)
    base = ids_ref[0]
    step = pl.program_id(0)
    per_shard = width // tile
    row_blocks = per_shard * full.shape[0]

    def copies():
        out = []
        for i, places in enumerate(plan):
            for at_col, shard, at_row, n_rows in places:
                out.append(
                    pltpu.make_async_copy(
                        src[i].at[:, pl.ds(at_col, width)],
                        full.at[shard, pl.ds(at_row, n_rows)],
                        sem.at[len(out)],
                    )
                )
        return out

    @pl.when(step == 0)
    def _():
        for copy in copies():
            copy.start()
        slots = slot_ref[...]
        for t in range(n_slots):
            masks[t] = jnp.where(slots == t, 1.0, 0.0).astype(BF16)
        masks[n_slots] = jnp.zeros(masks.shape[1:], BF16)
        for copy in copies():
            copy.wait()

    if with_anchor:
        anchor_out = jnp.zeros((rows, col_step * tile), F32)
        for p in range(full.shape[0]):
            at_row = pl.multiple_of(jnp.bitwise_xor(base, p) * width, width)
            anchor_out += jnp.dot(
                full[p], anchor_ref[0, pl.ds(at_row, width), :], preferred_element_type=F32
            )
        mean = jnp.broadcast_to(square_ref[0:1, :], (rows, rows)).T[:, 0:1]
        scale = lax.rsqrt(mean / (width * full.shape[0]) + EPS)

    for c in range(col_step):
        for t in range(n_slots):
            for s in range(per_list):
                where = 1 + (t * n_cols + step * col_step + c) * per_list + s
                block = ids_ref[where]
                kept = jnp.minimum(block, row_blocks - 1)
                shard = jnp.bitwise_xor(kept // per_shard, base)
                lane = pl.multiple_of((kept % per_shard) * tile, tile)
                mask = jnp.where(block < row_blocks, t, n_slots)
                piece = full[shard, :, pl.ds(lane, tile)] * masks[mask]
                at_col = (t * per_list + s) * tile
                pieces[:, at_col : at_col + tile] = piece
        tiles = tiles_ref[:, 0, c].reshape(n_slots * per_list * tile, tile)
        delta = jnp.dot(pieces[...], tiles, preferred_element_type=F32)
        cols = slice(c * tile, (c + 1) * tile)
        if with_anchor:
            own = (delta * scale).astype(BF16).astype(F32)
            out_ref[:, cols] = stream_ref[:, cols] + anchor_out[:, cols] * scale + own
        else:
            out_ref[:, cols] = delta.astype(BF16)


def products(ids, sources, plan, rows, slots, tiles, layer, col_step, extra=None):
    n_slots, _, n_cols, per_list, tile, _ = tiles.shape
    shards = 1 + max(place[1] for places in plan for place in places)
    out_width = n_cols * tile
    width = out_width
    with_anchor = extra is not None
    cfg = (
        len(sources), plan, with_anchor, n_slots, per_list, col_step, width, n_cols,
    )
    in_specs = [in_place()] * len(sources)
    in_specs += [
        whole(),
        pl.BlockSpec(
            (n_slots, 1, col_step, per_list, tile, tile), lambda i, ids: (0, layer, i, 0, 0, 0)
        ),
    ]
    operands = [*sources, slots, tiles]
    nbytes = rows * shards * width * 2 + n_slots * n_cols * per_list * tile * tile * 2
    flops = 2 * rows * out_width * n_slots * per_list * tile
    if with_anchor:
        anchor, stream, squares = extra
        in_specs += [
            pl.BlockSpec((1, shards * width, col_step * tile), lambda i, ids: (layer, 0, i)),
            pl.BlockSpec((rows, col_step * tile), lambda i, ids: (0, i)),
            whole(),
        ]
        operands += [anchor, stream, squares]
        nbytes += shards * width * out_width * 2
        flops += 2 * rows * out_width * shards * width
    n_copies = sum(len(places) for places in plan)
    return pl.pallas_call(
        functools.partial(product_kernel, cfg),
        out_shape=jax.ShapeDtypeStruct((rows, out_width), F32 if with_anchor else BF16),
        grid_spec=pltpu.PrefetchScalarGridSpec(
            num_scalar_prefetch=1,
            grid=(n_cols // col_step,),
            in_specs=in_specs,
            out_specs=pl.BlockSpec((rows, col_step * tile), lambda i, ids: (0, i)),
            scratch_shapes=[
                pltpu.VMEM((shards, rows, width), BF16),
                pltpu.VMEM((rows, n_slots * per_list * tile), BF16),
                pltpu.VMEM((n_slots + 1, rows, tile), BF16),
                pltpu.SemaphoreType.DMA((n_copies,)),
            ],
        ),
        compiler_params=params(dimension_semantics=("arbitrary",)),
        cost_estimate=pl.CostEstimate(flops=flops, bytes_accessed=nbytes, transcendentals=0),
        name="own_products" if with_anchor else "sent_products",
    )(ids, *operands)


def join_kernel(n_dest, last, total, *refs):
    partial_ref, back_ref, square_ref = refs[:3]
    rets = refs[3 : 3 + n_dest]
    rows = partial_ref.shape[0]
    cap = rets[0].shape[0]
    mean = jnp.broadcast_to(square_ref[0:1, :], (rows, rows)).T[:, 0:1]
    scale = lax.rsqrt(mean / total + EPS)
    delta = jnp.zeros(partial_ref.shape, F32)
    for d in range(n_dest):
        delta += jnp.dot(
            back_ref[:, d * cap : (d + 1) * cap], rets[d][...], preferred_element_type=F32
        )
    routed = (delta * scale).astype(BF16).astype(F32)
    stream = partial_ref[...] + routed
    if last:
        refs[3 + n_dest][...] = stream.astype(BF16)
        return
    gain_ref, stream_ref, y_ref, sum_ref = refs[3 + n_dest :]
    stream_ref[...] = stream
    y_ref[...] = (stream * gain_ref[...]).astype(BF16)
    squares = jnp.sum(stream * stream, axis=1, keepdims=True)
    sum_ref[...] = jnp.broadcast_to(squares, (rows, rows)).T[0:8, :]


def join(partial, back, squares, rets, gain, total):
    rows, width = partial.shape
    last = gain is None
    if last:
        out_shape = jax.ShapeDtypeStruct((rows, width), BF16)
        extra = []
    else:
        out_shape = [
            jax.ShapeDtypeStruct((rows, width), F32),
            jax.ShapeDtypeStruct((rows, width), BF16),
            jax.ShapeDtypeStruct((8, rows), F32),
        ]
        extra = [gain]
    return pl.pallas_call(
        functools.partial(join_kernel, len(rets), last, total),
        out_shape=out_shape,
        in_specs=[whole()] * (3 + len(rets) + len(extra)),
        out_specs=whole() if last else [whole()] * 3,
        compiler_params=params(),
        cost_estimate=pl.CostEstimate(
            flops=4 * rows * width, bytes_accessed=16 * rows * width, transcendentals=0
        ),
        name="join",
    )(partial, back, squares, *rets, *extra)


def body(hidden, norm_gain, anchor, delta_tiles, tile_rows, tenant):
    groups = lax.axis_size("group")
    tp_count = lax.axis_size("tp")
    my_group = lax.axis_index("group")
    my_tp = lax.axis_index("tp")
    rows, width = hidden.shape
    total = width * tp_count
    per_group, n_layers, n_cols, per_list, tile, _ = delta_tiles.shape
    cap = rows // 4
    n_dest = groups - 1
    offsets = list(range(1, groups))

    owner = tenant // per_group
    local = tenant % per_group
    dests = jnp.bitwise_xor(my_group, jnp.arange(1, groups, dtype=jnp.int32))
    to_dest = (owner[None, :] == dests[:, None]).astype(jnp.int32)
    rank = jnp.cumsum(to_dest, axis=1) - to_dest
    slot_of = jnp.arange(cap, dtype=jnp.int32)
    hot = (rank[:, None, :] == slot_of[None, :, None]) & (to_dest[:, None, :] > 0)
    hot = hot.reshape(n_dest * cap, rows)
    sel = hot.astype(BF16)
    back = hot.T.astype(BF16)
    labels = jnp.sum(jnp.where(hot, local[None, :] + 1, 0), axis=1).reshape(n_dest, 1, cap)
    got_labels = [swap(labels[i], "group", d) for i, d in enumerate(offsets)]
    got_slots = jnp.concatenate(got_labels, axis=1).reshape(n_dest * cap, 1) - 1
    got_slots = jnp.broadcast_to(got_slots, (n_dest * cap, tile))
    own_slots = jnp.broadcast_to(
        jnp.where(owner == my_group, local, -1)[:, None], (rows, tile)
    )

    stream = hidden.astype(F32)
    y = (stream * norm_gain[0][None, :]).astype(BF16)
    squares = jnp.broadcast_to(jnp.sum(stream * stream, axis=1)[None, :], (8, rows))

    pairwise = tp_count <= 8
    half = tp_count // 2 if pairwise else 1
    per_chunk = tp_count // half
    if pairwise:
        base = my_tp.reshape(1)
        own_plan = tuple(((0, p, 0, rows),) for p in range(tp_count))
    else:
        base = jnp.zeros((1,), jnp.int32)
        own_plan = (tuple((p * width, p, 0, rows) for p in range(tp_count)),)
    sent_plan = []
    for i in range(n_dest):
        for q in range(half):
            sent_plan.append(
                tuple(
                    (k * width, per_chunk * q + k, i * cap, cap) for k in range(per_chunk)
                )
            )
    sent_plan = tuple(sent_plan)

    for layer in range(n_layers):
        ids = jnp.concatenate([base, tile_rows[:, layer].reshape(-1)])
        far = {0: y}
        for q in range(1, half):
            far[q] = swap(y, "tp", 2 * q)
        shards = []
        sent = [[None] * half for _ in range(n_dest)]
        for q in range(half):
            if pairwise:
                chunk = [far[q], swap(far[q], "tp", 1)]
            else:
                chunk = [lax.all_gather(y, "tp", axis=1, tiled=True)]
            shards += chunk
            picked = pick_rows(sel, chunk, cap)
            for i, d in enumerate(offsets):
                sent[i][q] = swap(picked[i], "group", d)
        step = 1
        while step < tp_count:
            squares = squares + swap(squares, "tp", step)
            step *= 2
        partial = products(
            ids, shards, own_plan, rows, own_slots, delta_tiles, layer, 2,
            extra=(anchor, stream, squares),
        )
        got = [sent[i][q] for i in range(n_dest) for q in range(half)]
        answers = products(
            ids, got, sent_plan, n_dest * cap, got_slots, delta_tiles, layer, 1
        )
        rets = [
            swap(answers[i * cap : (i + 1) * cap], "group", d) for i, d in enumerate(offsets)
        ]
        if layer + 1 < n_layers:
            stream, y, squares = join(
                partial, back, squares, rets, norm_gain[layer + 1][None, :], total
            )
        else:
            updated = join(partial, back, squares, rets, None, total)
    return updated


def solution(mesh):
    return jax.shard_map(
        body,
        mesh=mesh,
        in_specs=(
            P("group", "tp"),
            P(None, "tp"),
            P(None, None, "tp"),
            P("group", None, "tp", None, None, None),
            P("group", None, "tp", None),
            P("group"),
        ),
        out_specs=P("group", "tp"),
        check_vma=False,
    )
```

```python
import functools

import jax
import jax.numpy as jnp
from jax import lax
from jax.experimental import pallas as pl
from jax.experimental.pallas import tpu as pltpu
from jax.sharding import PartitionSpec as P


F32 = jnp.float32
BF16 = jnp.bfloat16
EPS = 1e-05


def swap(value, axis, offset):
    size = lax.axis_size(axis)
    return lax.ppermute(value, axis, [(i, i ^ offset) for i in range(size)])


def params(mib, **kw):
    return pltpu.CompilerParams(vmem_limit_bytes=mib * 1024 * 1024, **kw)


def whole():
    return pl.BlockSpec(memory_space=pltpu.VMEM)


def in_place():
    return pl.BlockSpec(memory_space=pl.ANY)


def pick_kernel(n_dest, n_shards, *refs):
    sel_ref = refs[0]
    shard_refs = refs[1 : 1 + n_shards]
    out_refs = refs[1 + n_shards :]
    cap = out_refs[0].shape[0]
    width = shard_refs[0].shape[1]
    for s, shard in enumerate(shard_refs):
        rows = jnp.dot(sel_ref[...], shard[...], preferred_element_type=F32).astype(BF16)
        for d in range(n_dest):
            out_refs[d][:, s * width : (s + 1) * width] = rows[d * cap : (d + 1) * cap]


def pick_rows(sel, shards, cap):
    n_dest = sel.shape[0] // cap
    width = shards[0].shape[1] * len(shards)
    nbytes = sum(x.size for x in shards) * 2 + n_dest * cap * width * 2
    return pl.pallas_call(
        functools.partial(pick_kernel, n_dest, len(shards)),
        out_shape=[jax.ShapeDtypeStruct((cap, width), BF16)] * n_dest,
        in_specs=[whole()] * (1 + len(shards)),
        out_specs=[whole()] * n_dest,
        compiler_params=params(8),
        cost_estimate=pl.CostEstimate(
            flops=2 * sel.size * width, bytes_accessed=nbytes, transcendentals=0
        ),
        name="pick_rows",
    )(sel, *shards)


def product_kernel(cfg, ids_ref, *refs):
    n_in, plan, with_anchor, n_slots, per_list, col_step, width = cfg
    src = refs[:n_in]
    slot_ref, tiles_ref = refs[n_in], refs[n_in + 1]
    at = n_in + 2
    if with_anchor:
        anchor_ref, stream_ref, inverse_ref = refs[at : at + 3]
        out_ref, scale_ref = refs[at + 3 : at + 5]
        at += 5
    else:
        out_ref = refs[at]
        at += 1
    full, masks, sem = refs[at : at + 3]
    rows = full.shape[1]
    shards = full.shape[0] - 1
    group = n_slots * per_list
    tile = masks.shape[2]
    step = pl.program_id(0)
    per_shard = width // tile
    shift = per_shard.bit_length() - 1

    def copies():
        out = []
        for i, places in enumerate(plan):
            for at_col, shard, at_row, n_rows in places:
                out.append(
                    pltpu.make_async_copy(
                        src[i].at[:, pl.ds(at_col, width)],
                        full.at[shard, pl.ds(at_row, n_rows)],
                        sem.at[len(out)],
                    )
                )
        return out

    @pl.when(step == 0)
    def _():
        for copy in copies():
            copy.start()
        slots = slot_ref[...]
        for t in range(n_slots):
            masks[t] = jnp.where(slots == t, 1.0, 0.0).astype(BF16)
        full[shards, :, 0:tile] = jnp.zeros((rows, tile), BF16)
        for copy in copies():
            copy.wait()
        if with_anchor:
            squares = jnp.zeros((rows, tile), F32)
            for p in range(shards):
                for k in range(per_shard):
                    lanes = slice(k * tile, (k + 1) * tile)
                    value = full[p, :, lanes].astype(F32) * inverse_ref[p : p + 1, lanes]
                    squares += value * value
            mean = jnp.sum(squares, axis=1, keepdims=True) / (width * shards)
            scale_ref[...] = jnp.broadcast_to(lax.rsqrt(mean + EPS), (rows, tile))

    if with_anchor:
        base = ids_ref[0]
        anchor_out = jnp.zeros((rows, col_step * tile), F32)
        for p in range(shards):
            at_row = pl.multiple_of(jnp.bitwise_xor(base, p) * width, width)
            anchor_out += jnp.dot(
                full[p], anchor_ref[0, pl.ds(at_row, width), :], preferred_element_type=F32
            )
        scale = scale_ref[...]

    for c in range(col_step):
        delta = jnp.zeros((rows, tile), F32)
        for t in range(n_slots):
            parts = []
            for s in range(per_list):
                block = ids_ref[1 + (step * col_step + c) * group + t * per_list + s]
                shard = lax.shift_right_logical(block, shift)
                lane = pl.multiple_of(jnp.bitwise_and(block, per_shard - 1) * tile, tile)
                piece = full[shard, :, pl.ds(lane, tile)] * masks[t]
                parts.append(piece)
            delta += jnp.dot(jnp.concatenate(parts, axis=1), tiles_ref[t, 0, c].reshape(per_list * tile, tile), preferred_element_type=F32)
        cols = slice(c * tile, (c + 1) * tile)
        if with_anchor:
            own = (delta * scale).astype(BF16).astype(F32)
            out_ref[:, cols] = stream_ref[:, cols] + anchor_out[:, cols] * scale + own
        else:
            out_ref[:, cols] = delta.astype(BF16)


def products(ids, sources, plan, rows, slots, tiles, layer, col_step, extra=None):
    n_slots, _, n_cols, per_list, tile, _ = tiles.shape
    shards = 1 + max(place[1] for places in plan for place in places)
    width = n_cols * tile
    with_anchor = extra is not None
    cfg = (len(sources), plan, with_anchor, n_slots, per_list, col_step, width)
    in_specs = [in_place()] * len(sources)
    in_specs += [
        whole(),
        pl.BlockSpec(
            (n_slots, 1, col_step, per_list, tile, tile), lambda i, ids: (0, layer, i, 0, 0, 0)
        ),
    ]
    operands = [*sources, slots, tiles]
    out_shape = jax.ShapeDtypeStruct((rows, width), F32 if with_anchor else BF16)
    out_specs = pl.BlockSpec((rows, col_step * tile), lambda i, ids: (0, i))
    nbytes = rows * shards * width * 2 + n_slots * n_cols * per_list * tile * tile * 2
    flops = 2 * rows * width * n_slots * per_list * tile
    if with_anchor:
        in_specs += [
            pl.BlockSpec((1, shards * width, col_step * tile), lambda i, ids: (layer, 0, i)),
            pl.BlockSpec((rows, col_step * tile), lambda i, ids: (0, i)),
            whole(),
        ]
        operands += list(extra)
        out_shape = [out_shape, jax.ShapeDtypeStruct((rows, tile), F32)]
        out_specs = [out_specs, pl.BlockSpec((rows, tile), lambda i, ids: (0, 0))]
        nbytes += shards * width * width * 2
        flops += 2 * rows * width * shards * width
    n_copies = sum(len(places) for places in plan)
    return pl.pallas_call(
        functools.partial(product_kernel, cfg),
        out_shape=out_shape,
        grid_spec=pltpu.PrefetchScalarGridSpec(
            num_scalar_prefetch=1,
            grid=(n_cols // col_step,),
            in_specs=in_specs,
            out_specs=out_specs,
            scratch_shapes=[
                pltpu.VMEM((shards + 1, rows, width), BF16),
                pltpu.VMEM((n_slots, rows, tile), BF16),
                pltpu.SemaphoreType.DMA((n_copies,)),
            ],
        ),
        compiler_params=params(44, dimension_semantics=("arbitrary",)),
        cost_estimate=pl.CostEstimate(flops=flops, bytes_accessed=nbytes, transcendentals=0),
        name="own_products" if with_anchor else "sent_products",
    )(ids, *operands)


def join_kernel(n_dest, last, *refs):
    partial_ref, back_ref, scale_ref = refs[:3]
    rets = refs[3 : 3 + n_dest]
    cap = rets[0].shape[0]
    tile = scale_ref.shape[1]
    delta = jnp.zeros(partial_ref.shape, F32)
    for d in range(n_dest):
        delta += jnp.dot(
            back_ref[:, d * cap : (d + 1) * cap], rets[d][...], preferred_element_type=F32
        )
    scale = scale_ref[...]
    for k in range(partial_ref.shape[1] // tile):
        cols = slice(k * tile, (k + 1) * tile)
        routed = (delta[:, cols] * scale).astype(BF16).astype(F32)
        stream = partial_ref[:, cols] + routed
        if last:
            refs[3 + n_dest][:, cols] = stream.astype(BF16)
        else:
            gain_ref, stream_ref, y_ref = refs[3 + n_dest :]
            stream_ref[:, cols] = stream
            y_ref[:, cols] = (stream * gain_ref[:, cols]).astype(BF16)


def join(partial, back, scale, rets, gain):
    rows, width = partial.shape
    last = gain is None
    if last:
        out_shape = jax.ShapeDtypeStruct((rows, width), BF16)
        extra = []
    else:
        out_shape = [
            jax.ShapeDtypeStruct((rows, width), F32),
            jax.ShapeDtypeStruct((rows, width), BF16),
        ]
        extra = [gain]
    return pl.pallas_call(
        functools.partial(join_kernel, len(rets), last),
        out_shape=out_shape,
        in_specs=[whole()] * (3 + len(rets) + len(extra)),
        out_specs=whole() if last else [whole()] * 2,
        compiler_params=params(8),
        cost_estimate=pl.CostEstimate(
            flops=4 * rows * width, bytes_accessed=16 * rows * width, transcendentals=0
        ),
        name="join",
    )(partial, back, scale, *rets, *extra)


def gather_gains(norm_gain, pairwise):
    n_layers, width = norm_gain.shape
    count = lax.axis_size("tp")
    if not pairwise:
        gains = lax.all_gather(norm_gain, "tp", axis=1, tiled=True)
        return gains.reshape(n_layers, count, width)
    gains = norm_gain[:, None, :]
    step = 1
    while step < count:
        gains = jnp.concatenate([gains, swap(gains, "tp", step)], axis=1)
        step *= 2
    return gains


def body(hidden, norm_gain, anchor, delta_tiles, tile_rows, tenant):
    groups = lax.axis_size("group")
    tp_count = lax.axis_size("tp")
    my_group = lax.axis_index("group")
    my_tp = lax.axis_index("tp")
    rows, width = hidden.shape
    per_group, n_layers, _, _, tile, _ = delta_tiles.shape
    row_blocks = width * tp_count // tile
    per_shard = width // tile
    cap = rows // 4
    n_dest = groups - 1
    offsets = list(range(1, groups))
    pairwise = tp_count == 8

    stream = hidden.astype(F32)
    y = (stream * norm_gain[0][None, :]).astype(BF16)

    owner = tenant // per_group
    local = tenant % per_group
    dests = jnp.bitwise_xor(my_group, jnp.arange(1, groups, dtype=jnp.int32))
    to_dest = (owner[None, :] == dests[:, None]).astype(jnp.int32)
    rank = jnp.cumsum(to_dest, axis=1) - to_dest
    slot_of = jnp.arange(cap, dtype=jnp.int32)
    hot = (rank[:, None, :] == slot_of[None, :, None]) & (to_dest[:, None, :] > 0)
    hot = hot.reshape(n_dest * cap, rows)
    sel = hot.astype(BF16)
    back = hot.T.astype(BF16)
    labels = jnp.sum(jnp.where(hot, local[None, :] + 1, 0), axis=1).reshape(n_dest, 1, cap)
    got_labels = [swap(labels[i], "group", d) for i, d in enumerate(offsets)]
    got_slots = jnp.concatenate(got_labels, axis=1).reshape(n_dest * cap, 1) - 1
    got_slots = jnp.broadcast_to(got_slots, (n_dest * cap, tile))
    own_slots = jnp.broadcast_to(
        jnp.where(owner == my_group, local, -1)[:, None], (rows, tile)
    )

    base = my_tp if pairwise else jnp.zeros((), jnp.int32)
    blocks = jnp.bitwise_xor(tile_rows, base * per_shard)
    blocks = jnp.where(tile_rows < row_blocks, blocks, row_blocks)
    blocks = blocks.transpose(1, 2, 0, 3).reshape(n_layers, -1)
    ids_of = jnp.concatenate([jnp.full((n_layers, 1), base, jnp.int32), blocks], axis=1)
    inverse = 1.0 / gather_gains(norm_gain, pairwise)

    if pairwise:
        chunks = CHUNKS
        own_plan = tuple(((0, p, 0, rows),) for p in range(tp_count))
    else:
        chunks = (tuple(range(tp_count)),)
        own_plan = (tuple((p * width, p, 0, rows) for p in range(tp_count)),)
    sent_plan = tuple(
        tuple((k * width, p, i * cap, cap) for k, p in enumerate(chunk))
        for i in range(n_dest)
        for chunk in chunks
    )

    for layer in range(n_layers):
        ids = ids_of[layer]
        if pairwise:
            shards = gather_rows(y)
            parts = [[shards[p] for p in chunk] for chunk in chunks]
        else:
            shards = [lax.all_gather(y, "tp", axis=1, tiled=True)]
            parts = [shards]
        sent = [[None] * len(chunks) for _ in range(n_dest)]
        for q, part in enumerate(parts):
            picked = pick_rows(sel, part, cap)
            for i, d in enumerate(offsets):
                sent[i][q] = swap(picked[i], "group", d)
        partial, scale = products(
            ids, shards, own_plan, rows, own_slots, delta_tiles, layer, 2,
            extra=(anchor, stream, inverse[layer]),
        )
        got = [sent[i][q] for i in range(n_dest) for q in range(len(chunks))]
        answers = products(ids, got, sent_plan, n_dest * cap, got_slots, delta_tiles, layer, 2)
        rets = [swap(answers[i * cap : (i + 1) * cap], "group", d) for i, d in enumerate(offsets)]
        if layer + 1 < n_layers:
            gain = norm_gain[layer + 1][None, :]
            stream, y = join(partial, back, scale, rets, gain)
        else:
            updated = join(partial, back, scale, rets, None)
    return updated


CHUNKS = ((0, 1, 2, 4), (5, 6, 3, 7))


def gather_rows(y):
    near = {0: y}
    near[4] = swap(y, "tp", 4)
    near[2] = swap(y, "tp", 2)
    near[1] = swap(y, "tp", 1)
    near[6] = swap(near[4], "tp", 2)
    near[5] = swap(near[4], "tp", 1)
    near[3] = swap(near[2], "tp", 1)
    near[7] = swap(near[5], "tp", 2)
    return [near[p] for p in range(8)]


def solution(mesh):
    return jax.shard_map(
        body,
        mesh=mesh,
        in_specs=(
            P("group", "tp"),
            P(None, "tp"),
            P(None, None, "tp"),
            P("group", None, "tp", None, None, None),
            P("group", None, "tp", None),
            P("group"),
        ),
        out_specs=P("group", "tp"),
        check_vma=False,
    )
```

```python
import functools

import jax
import jax.numpy as jnp
from jax import lax
from jax.experimental import pallas as pl
from jax.experimental.pallas import tpu as pltpu
from jax.sharding import PartitionSpec as P


F32 = jnp.float32
BF16 = jnp.bfloat16
EPS = 1e-05


def swap(value, axis, offset):
    size = lax.axis_size(axis)
    return lax.ppermute(value, axis, [(i, i ^ offset) for i in range(size)])


def params(mib, **kw):
    return pltpu.CompilerParams(vmem_limit_bytes=mib * 1024 * 1024, **kw)


def whole():
    return pl.BlockSpec(memory_space=pltpu.VMEM)


def in_place():
    return pl.BlockSpec(memory_space=pl.ANY)


def pick_kernel(n_dest, n_shards, *refs):
    sel_ref = refs[0]
    shard_refs = refs[1 : 1 + n_shards]
    out_refs = refs[1 + n_shards :]
    cap = out_refs[0].shape[0]
    at = 0
    for shard in shard_refs:
        width = shard.shape[1]
        rows = jnp.dot(sel_ref[...], shard[...], preferred_element_type=F32).astype(BF16)
        for d in range(n_dest):
            out_refs[d][:, at : at + width] = rows[d * cap : (d + 1) * cap]
        at += width


def pick_rows(sel, shards, cap):
    n_dest = sel.shape[0] // cap
    width = sum(x.shape[1] for x in shards)
    nbytes = sum(x.size for x in shards) * 2 + n_dest * cap * width * 2
    return pl.pallas_call(
        functools.partial(pick_kernel, n_dest, len(shards)),
        out_shape=[jax.ShapeDtypeStruct((cap, width), BF16)] * n_dest,
        in_specs=[whole()] * (1 + len(shards)),
        out_specs=[whole()] * n_dest,
        compiler_params=params(8),
        cost_estimate=pl.CostEstimate(
            flops=2 * sel.size * width, bytes_accessed=nbytes, transcendentals=0
        ),
        name="pick_rows",
    )(sel, *shards)


def square_sum(total, x_ref, inverse_ref, p, tile):
    for k in range(inverse_ref.shape[1] // tile):
        lanes = slice(k * tile, (k + 1) * tile)
        value = x_ref[:, lanes].astype(F32) * inverse_ref[p : p + 1, lanes]
        total += value * value
    return total


def early_kernel(part, has_prior, tile, ids_ref, *refs):
    xs = refs[: len(part)]
    anchor_ref = refs[len(part)]
    prior = refs[len(part) + 1 : -1]
    sum_ref = refs[-1]
    step = pl.program_id(0)
    width = anchor_ref.shape[2]
    cols = min(2 * tile, width)
    for k in range(len(part)):

        @pl.when(step == k)
        def _(k=k):
            x = xs[k][...]
            for n in range(0, width, cols):
                lanes = slice(n, n + cols)
                value = jnp.dot(x, anchor_ref[0, :, lanes], preferred_element_type=F32)
                if k > 0:
                    value += sum_ref[:, lanes]
                elif has_prior:
                    value += prior[0][:, lanes]
                sum_ref[:, lanes] = value


def early_products(row_of, part, xs, anchor, prior, layer, tile):
    rows, width = xs[0].shape
    return pl.pallas_call(
        functools.partial(early_kernel, part, bool(prior), tile),
        out_shape=jax.ShapeDtypeStruct((rows, width), F32),
        grid_spec=pltpu.PrefetchScalarGridSpec(
            num_scalar_prefetch=1,
            grid=(len(part),),
            in_specs=[whole()] * len(part)
            + [pl.BlockSpec((1, width, width), lambda i, ids: (layer, ids[i], 0))]
            + [whole()] * len(prior),
            out_specs=pl.BlockSpec((rows, width), lambda i, ids: (0, 0)),
        ),
        compiler_params=params(32, dimension_semantics=("arbitrary",)),
        cost_estimate=pl.CostEstimate(
            flops=2 * rows * width * width * len(part),
            bytes_accessed=2 * width * width * len(part),
            transcendentals=0,
        ),
        name="early_products",
    )(row_of, *xs, anchor, *prior)


def stage_kernel(layer, tiles_ref, out_ref, sem):
    copies = [
        pltpu.make_async_copy(tiles_ref.at[t, layer], out_ref.at[t], sem.at[t])
        for t in range(out_ref.shape[0])
    ]
    for copy in copies:
        copy.start()
    for copy in copies:
        copy.wait()


def stage_tiles(tiles, layer):
    shape = tiles.shape[:1] + tiles.shape[2:]
    return pl.pallas_call(
        functools.partial(stage_kernel, layer),
        out_shape=jax.ShapeDtypeStruct(shape, BF16),
        in_specs=[in_place()],
        out_specs=whole(),
        scratch_shapes=[pltpu.SemaphoreType.DMA((shape[0],))],
        compiler_params=params(40),
        cost_estimate=pl.CostEstimate(
            flops=0, bytes_accessed=tiles.size * 2, transcendentals=0
        ),
        name="stage_tiles",
    )(tiles)


def product_kernel(cfg, ids_ref, *refs):
    n_in, plan, label_plan, parts, has_prior, layer, n_cols, col_step, width = cfg
    src = refs[:n_in]
    tiles_ref = refs[n_in]
    at = n_in + 1
    with_anchor = parts is not None
    if with_anchor:
        anchor_ref, stream_ref, inverse_ref = refs[at : at + 3]
        at += 3
        if has_prior:
            sum_ref = refs[at]
            at += 1
        out_ref, scale_ref = refs[at : at + 2]
        at += 2
    else:
        out_ref = refs[at]
        at += 1
    full, labels, masks, sem = refs[at : at + 4]
    rows = full.shape[1]
    shards = full.shape[0] - 1
    n_slots, _, per_list, tile = tiles_ref.shape[:4]
    group = n_slots * per_list
    per_shard = width // tile
    shift = per_shard.bit_length() - 1

    copies = []
    for i, places in enumerate(plan):
        for at_col, shard, at_row, n_rows in places:
            copies.append(
                pltpu.make_async_copy(
                    src[i].at[:, pl.ds(at_col, width)],
                    full.at[shard, pl.ds(at_row, n_rows)],
                    sem.at[len(copies)],
                )
            )
    for i, at_col, at_row, n_rows in label_plan:
        copies.append(
            pltpu.make_async_copy(
                src[i].at[:, pl.ds(at_col, tile)],
                labels.at[pl.ds(at_row, n_rows)],
                sem.at[len(copies)],
            )
        )
    weights = []
    if with_anchor:
        anchor_buf, anchor_sem = refs[at + 4 : at + 6]
        at_row = 0
        for k, part in enumerate(parts):
            n_rows = len(part) * width
            row = pl.multiple_of(ids_ref[part[0]] * width, width) if len(part) == 1 else 0
            weights.append(
                pltpu.make_async_copy(
                    anchor_ref.at[layer, pl.ds(row, n_rows)],
                    anchor_buf.at[pl.ds(at_row, n_rows)],
                    anchor_sem.at[k],
                )
            )
            at_row += n_rows

    for copy in copies + weights:
        copy.start()
    full[shards, :, 0:tile] = jnp.zeros((rows, tile), BF16)
    for copy in copies:
        copy.wait()
    label = labels[...].astype(F32)
    for t in range(n_slots):
        masks[t] = jnp.where(label == t + 1, 1.0, 0.0).astype(BF16)
    if with_anchor:
        squares = jnp.zeros((rows, tile), F32)
        for p in range(shards):
            squares = square_sum(squares, full.at[p], inverse_ref, p, tile)
        mean = jnp.sum(squares, axis=1, keepdims=True) / (width * shards)
        scale_ref[...] = jnp.broadcast_to(lax.rsqrt(mean + EPS), (rows, tile))
        for copy in weights:
            copy.wait()
        step_cols = col_step * tile
        for n in range(0, width, step_cols):
            lanes = slice(n, n + step_cols)
            anchor_out = jnp.zeros((rows, step_cols), F32)
            for k, p in enumerate([p for part in parts for p in part]):
                anchor_out += jnp.dot(
                    full[p],
                    anchor_buf[k * width : (k + 1) * width, lanes],
                    preferred_element_type=F32,
                )
            if has_prior:
                anchor_out += sum_ref[:, lanes]
            for k in range(0, step_cols, tile):
                out = anchor_out[:, k : k + tile] * scale_ref[...]
                out_ref[:, n + k : n + k + tile] = stream_ref[:, n + k : n + k + tile] + out

    def block_step(step, carry):
        for k in range(col_step):
            c = step * col_step + k
            delta = jnp.zeros((rows, tile), F32)
            for t in range(n_slots):
                pieces = []
                for s in range(per_list):
                    block = ids_ref[shards + c * group + t * per_list + s]
                    shard = lax.shift_right_logical(block, shift)
                    lane = pl.multiple_of(jnp.bitwise_and(block, per_shard - 1) * tile, tile)
                    pieces.append(full[shard, :, pl.ds(lane, tile)] * masks[t])
                delta += jnp.dot(
                    jnp.concatenate(pieces, axis=1),
                    tiles_ref[t, c].reshape(per_list * tile, tile),
                    preferred_element_type=F32,
                )
            cols = pl.ds(pl.multiple_of(c * tile, tile), tile)
            if with_anchor:
                out_ref[:, cols] += (delta * scale_ref[...]).astype(BF16).astype(F32)
            else:
                out_ref[:, cols] = delta.astype(BF16)
        return carry

    lax.fori_loop(0, n_cols // col_step, block_step, 0)


def products(
    ids, sources, plan, label_plan, rows, tiles, layer, col_step,
    parts=None, anchor=None, stream=None, inverse=None, prior=(),
):
    n_slots, n_cols, per_list, tile, _ = tiles.shape
    shards = 1 + max(place[1] for places in plan for place in places)
    width = n_cols * tile
    with_anchor = parts is not None
    cfg = (
        len(sources), plan, label_plan, parts, bool(prior), layer, n_cols, col_step, width,
    )
    in_specs = [in_place()] * len(sources) + [whole()]
    operands = [*sources, tiles]
    out_shape = jax.ShapeDtypeStruct((rows, width), F32 if with_anchor else BF16)
    nbytes = rows * shards * width * 2 + n_slots * n_cols * per_list * tile * tile * 2
    flops = 2 * rows * width * n_slots * per_list * tile
    n_copies = sum(len(places) for places in plan) + len(label_plan)
    scratch = [
        pltpu.VMEM((shards + 1, rows, width), BF16),
        pltpu.VMEM((rows, tile), BF16),
        pltpu.VMEM((n_slots, rows, tile), BF16),
        pltpu.SemaphoreType.DMA((n_copies,)),
    ]
    if with_anchor:
        n_late = sum(len(part) for part in parts)
        in_specs += [in_place()] + [whole()] * (2 + len(prior))
        operands += [anchor, stream, inverse, *prior]
        out_shape = [out_shape, jax.ShapeDtypeStruct((rows, tile), F32)]
        scratch += [
            pltpu.VMEM((n_late * width, width), BF16),
            pltpu.SemaphoreType.DMA((len(parts),)),
        ]
        nbytes += n_late * width * width * 2
        flops += 2 * rows * width * n_late * width
    return pl.pallas_call(
        functools.partial(product_kernel, cfg),
        out_shape=out_shape,
        in_specs=[pl.BlockSpec(memory_space=pltpu.SMEM)] + in_specs,
        out_specs=[whole()] * 2 if with_anchor else whole(),
        scratch_shapes=scratch,
        compiler_params=params(32),
        cost_estimate=pl.CostEstimate(flops=flops, bytes_accessed=nbytes, transcendentals=0),
        name="own_products" if with_anchor else "sent_products",
    )(ids, *operands)


def join_kernel(n_dest, last, *refs):
    partial_ref, back_ref, scale_ref = refs[:3]
    rets = refs[3 : 3 + n_dest]
    cap = rets[0].shape[0]
    tile = scale_ref.shape[1]
    delta = jnp.zeros(partial_ref.shape, F32)
    for d in range(n_dest):
        delta += jnp.dot(
            back_ref[:, d * cap : (d + 1) * cap], rets[d][...], preferred_element_type=F32
        )
    scale = scale_ref[...]
    for k in range(partial_ref.shape[1] // tile):
        cols = slice(k * tile, (k + 1) * tile)
        routed = (delta[:, cols] * scale).astype(BF16).astype(F32)
        stream = partial_ref[:, cols] + routed
        if last:
            refs[3 + n_dest][:, cols] = stream.astype(BF16)
        else:
            gain_ref, stream_ref, y_ref = refs[3 + n_dest :]
            stream_ref[:, cols] = stream
            y_ref[:, cols] = (stream * gain_ref[:, cols]).astype(BF16)


def join(partial, back, scale, rets, gain):
    rows, width = partial.shape
    last = gain is None
    if last:
        out_shape = jax.ShapeDtypeStruct((rows, width), BF16)
        extra = []
    else:
        out_shape = [
            jax.ShapeDtypeStruct((rows, width), F32),
            jax.ShapeDtypeStruct((rows, width), BF16),
        ]
        extra = [gain]
    return pl.pallas_call(
        functools.partial(join_kernel, len(rets), last),
        out_shape=out_shape,
        in_specs=[whole()] * (3 + len(rets) + len(extra)),
        out_specs=whole() if last else [whole()] * 2,
        compiler_params=params(8),
        cost_estimate=pl.CostEstimate(
            flops=4 * rows * width, bytes_accessed=16 * rows * width, transcendentals=0
        ),
        name="join",
    )(partial, back, scale, *rets, *extra)


def gather_gains(norm_gain, pairwise):
    n_layers, width = norm_gain.shape
    count = lax.axis_size("tp")
    if not pairwise:
        gains = lax.all_gather(norm_gain, "tp", axis=1, tiled=True)
        return gains.reshape(n_layers, count, width)
    gains = norm_gain[:, None, :]
    step = 1
    while step < count:
        gains = jnp.concatenate([gains, swap(gains, "tp", step)], axis=1)
        step *= 2
    return gains


def body(hidden, norm_gain, anchor, delta_tiles, tile_rows, tenant):
    groups = lax.axis_size("group")
    tp_count = lax.axis_size("tp")
    my_group = lax.axis_index("group")
    my_tp = lax.axis_index("tp")
    rows, width = hidden.shape
    per_group, n_layers, _, _, tile, _ = delta_tiles.shape
    row_blocks = width * tp_count // tile
    per_shard = width // tile
    cap = rows // 4
    n_dest = groups - 1
    offsets = list(range(1, groups))
    pairwise = tp_count == 8

    stream = hidden.astype(F32)
    y = (stream * norm_gain[0][None, :]).astype(BF16)

    owner = tenant // per_group
    local = tenant % per_group
    dests = jnp.bitwise_xor(my_group, jnp.arange(1, groups, dtype=jnp.int32))
    to_dest = (owner[None, :] == dests[:, None]).astype(jnp.int32)
    rank = jnp.cumsum(to_dest, axis=1) - to_dest
    slot_of = jnp.arange(cap, dtype=jnp.int32)
    hot = (rank[:, None, :] == slot_of[None, :, None]) & (to_dest[:, None, :] > 0)
    hot = hot.reshape(n_dest * cap, rows)
    sel = hot.astype(BF16)
    back = hot.T.astype(BF16)
    label = jnp.broadcast_to((local + 1)[:, None], (rows, tile)).astype(BF16)
    own_label = jnp.where((owner == my_group)[:, None], label, 0.0).astype(BF16)

    base = my_tp if pairwise else jnp.zeros((), jnp.int32)
    blocks = jnp.bitwise_xor(tile_rows, base * per_shard)
    blocks = jnp.where(tile_rows < row_blocks, blocks, row_blocks)
    blocks = blocks.transpose(1, 2, 0, 3).reshape(n_layers, -1)
    shard_of = jnp.bitwise_xor(base, jnp.arange(tp_count, dtype=jnp.int32))
    shard_of = jnp.broadcast_to(shard_of[None, :], (n_layers, tp_count))
    ids_of = jnp.concatenate([shard_of, blocks], axis=1)
    inverse = 1.0 / gather_gains(norm_gain, pairwise)

    if pairwise:
        chunks, early, late = CHUNKS, EARLY, tuple((p,) for p in LATE)
        own_plan = tuple(((0, p, 0, rows),) for p in range(tp_count))
        near_plan = (tuple((p * width, p, 0, cap) for p in range(tp_count)),)
    else:
        chunks = (tuple(range(tp_count)),)
        early, late = (), chunks
        own_plan = (tuple((p * width, p, 0, rows) for p in range(tp_count)),)
        near_plan = (tuple((p * width, p, 0, cap) for p in range(tp_count)),)
    far_plan = tuple(
        tuple((k * width, p, i * cap, cap) for k, p in enumerate(chunk))
        for i in range(1, n_dest)
        for chunk in chunks
    )
    sent_plan = near_plan + far_plan
    n_chunks = len(chunks)
    own_labels = ((len(own_plan), 0, 0, rows),)
    sent_labels = ((0, width * tp_count, 0, cap),) + tuple(
        (1 + (i - 1) * n_chunks, len(chunks[0]) * width, i * cap, cap)
        for i in range(1, n_dest)
    )
    own_plan += ((),)

    for layer in range(n_layers):
        ids = ids_of[layer]
        if pairwise:
            shards = gather_rows(y)
            split = [[shards[p] for p in chunk] for chunk in chunks]
        else:
            shards = [lax.all_gather(y, "tp", axis=1, tiled=True)]
            split = [shards]
        far = [[] for _ in range(n_dest)]
        for q, xs in enumerate(split):
            if q == 0:
                xs = xs + [label]
            picked = pick_rows(sel[cap:], xs, cap)
            for i, d in enumerate(offsets[1:]):
                far[i + 1].append(swap(picked[i], "group", d))
        (picked,) = pick_rows(sel[:cap], shards + [label], cap)
        got = [swap(picked, "group", 1)]
        for pieces in far[1:]:
            got += pieces
        tiles = stage_tiles(delta_tiles, layer)
        prior = ()
        for part in early:
            row_of = jnp.stack([jnp.bitwise_xor(base, p) for p in part])
            prior = early_products(
                row_of, part, [shards[p] for p in part], anchor, prior, layer, tile
            )
            prior = (prior,)
        partial, scale = products(
            ids, shards + [own_label], own_plan, own_labels, rows, tiles,
            layer, 2,
            parts=late, anchor=anchor, stream=stream, inverse=inverse[layer],
            prior=prior,
        )
        answers = products(
            ids, got, sent_plan, sent_labels, n_dest * cap, tiles, layer, 2
        )
        rets = [
            swap(answers[i * cap : (i + 1) * cap], "group", d)
            for i, d in enumerate(offsets)
        ]
        if layer + 1 < n_layers:
            gain = norm_gain[layer + 1][None, :]
            stream, y = join(partial, back, scale, rets, gain)
        else:
            updated = join(partial, back, scale, rets, None)
    return updated


CHUNKS = ((0, 1, 2, 4), (5, 6), (3, 7))
EARLY = ((0, 1), (2, 4), (5, 6))
LATE = (3, 7)


def gather_rows(y):
    near = {0: y}
    near[4] = swap(y, "tp", 4)
    near[2] = swap(y, "tp", 2)
    near[1] = swap(y, "tp", 1)
    near[6] = swap(near[4], "tp", 2)
    near[5] = swap(near[4], "tp", 1)
    near[3] = swap(near[2], "tp", 1)
    near[7] = swap(near[5], "tp", 2)
    return [near[p] for p in range(8)]


def solution(mesh):
    return jax.shard_map(
        body,
        mesh=mesh,
        in_specs=(
            P("group", "tp"),
            P(None, "tp"),
            P(None, None, "tp"),
            P("group", None, "tp", None, None, None),
            P("group", None, "tp", None),
            P("group"),
        ),
        out_specs=P("group", "tp"),
        check_vma=False,
    )
```

```python
import functools

import jax
import jax.numpy as jnp
from jax import lax
from jax.experimental import pallas as pl
from jax.experimental.pallas import tpu as pltpu
from jax.sharding import PartitionSpec as P


F32 = jnp.float32
BF16 = jnp.bfloat16
EPS = 1e-05


def swap(value, axis, offset):
    size = lax.axis_size(axis)
    return lax.ppermute(value, axis, [(i, i ^ offset) for i in range(size)])


def params(mib, **kw):
    return pltpu.CompilerParams(vmem_limit_bytes=mib * 1024 * 1024, **kw)


def whole():
    return pl.BlockSpec(memory_space=pltpu.VMEM)


def in_place():
    return pl.BlockSpec(memory_space=pl.ANY)


def pick_kernel(n_dest, n_shards, *refs):
    sel_ref = refs[0]
    shard_refs = refs[1 : 1 + n_shards]
    out_refs = refs[1 + n_shards :]
    cap = out_refs[0].shape[0]
    at = 0
    for shard in shard_refs:
        width = shard.shape[1]
        rows = jnp.dot(sel_ref[...], shard[...], preferred_element_type=F32).astype(BF16)
        for d in range(n_dest):
            out_refs[d][:, at : at + width] = rows[d * cap : (d + 1) * cap]
        at += width


def pick_rows(sel, shards, cap):
    n_dest = sel.shape[0] // cap
    width = sum(x.shape[1] for x in shards)
    nbytes = sum(x.size for x in shards) * 2 + n_dest * cap * width * 2
    return pl.pallas_call(
        functools.partial(pick_kernel, n_dest, len(shards)),
        out_shape=[jax.ShapeDtypeStruct((cap, width), BF16)] * n_dest,
        in_specs=[whole()] * (1 + len(shards)),
        out_specs=[whole()] * n_dest,
        compiler_params=params(8),
        cost_estimate=pl.CostEstimate(
            flops=2 * sel.size * width, bytes_accessed=nbytes, transcendentals=0
        ),
        name="pick_rows",
    )(sel, *shards)


def square_sum(total, x_ref, inverse_ref, p, tile):
    for k in range(inverse_ref.shape[1] // tile):
        lanes = slice(k * tile, (k + 1) * tile)
        value = x_ref[:, lanes].astype(F32) * inverse_ref[p : p + 1, lanes]
        total += value * value
    return total


def early_kernel(squared, has_prior, n_part, tile, ids_ref, *refs):
    xs = refs[:n_part]
    anchor_ref, inverse_ref = refs[n_part : n_part + 2]
    prior = refs[n_part + 2 : -2]
    sum_ref, square_ref = refs[-2:]
    step = pl.program_id(0)
    width = anchor_ref.shape[2]
    cols = min(2 * tile, width)
    for k in range(n_part):

        @pl.when(step == k)
        def _(k=k):
            x = xs[k][...]
            for n in range(0, width, cols):
                lanes = slice(n, n + cols)
                value = jnp.dot(x, anchor_ref[0, :, lanes], preferred_element_type=F32)
                if k > 0:
                    value += sum_ref[:, lanes]
                elif has_prior:
                    value += prior[0][:, lanes]
                sum_ref[:, lanes] = value

    @pl.when(step == 0)
    def _():
        squares = prior[1][...] if has_prior else jnp.zeros(square_ref.shape, F32)
        for k, p in squared:
            x_ref = xs[k]
            squares = square_sum(squares, x_ref, inverse_ref, p, tile)
        square_ref[...] = squares


def early_products(row_of, xs, n_part, squared, anchor, inverse, prior, layer, tile):
    rows, width = xs[0].shape
    whole_rows = pl.BlockSpec((rows, width), lambda i, ids: (0, 0))
    whole_tile = pl.BlockSpec((rows, tile), lambda i, ids: (0, 0))
    return pl.pallas_call(
        functools.partial(early_kernel, squared, bool(prior), n_part, tile),
        out_shape=[
            jax.ShapeDtypeStruct((rows, width), F32),
            jax.ShapeDtypeStruct((rows, tile), F32),
        ],
        grid_spec=pltpu.PrefetchScalarGridSpec(
            num_scalar_prefetch=1,
            grid=(n_part,),
            in_specs=[whole()] * len(xs)
            + [pl.BlockSpec((1, width, width), lambda i, ids: (layer, ids[i], 0))]
            + [whole()] * (1 + len(prior)),
            out_specs=[whole_rows, whole_tile],
        ),
        compiler_params=params(32, dimension_semantics=("arbitrary",)),
        cost_estimate=pl.CostEstimate(
            flops=2 * rows * width * width * n_part,
            bytes_accessed=2 * width * width * n_part,
            transcendentals=0,
        ),
        name="early_products",
    )(row_of, *xs, anchor, inverse, *prior)


def stage_kernel(layer, tiles_ref, out_ref, sem):
    copies = [
        pltpu.make_async_copy(tiles_ref.at[t, layer], out_ref.at[t], sem.at[t])
        for t in range(out_ref.shape[0])
    ]
    for copy in copies:
        copy.start()
    for copy in copies:
        copy.wait()


def stage_tiles(tiles, layer):
    shape = tiles.shape[:1] + tiles.shape[2:]
    return pl.pallas_call(
        functools.partial(stage_kernel, layer),
        out_shape=jax.ShapeDtypeStruct(shape, BF16),
        in_specs=[in_place()],
        out_specs=whole(),
        scratch_shapes=[pltpu.SemaphoreType.DMA((shape[0],))],
        compiler_params=params(40),
        cost_estimate=pl.CostEstimate(
            flops=0, bytes_accessed=tiles.size * 2, transcendentals=0
        ),
        name="stage_tiles",
    )(tiles)


def product_kernel(cfg, ids_ref, *refs):
    n_in, plan, label_plan, parts, has_prior, done, layer, n_cols, col_step, width = cfg
    src = refs[:n_in]
    tiles_ref = refs[n_in]
    at = n_in + 1
    with_anchor = parts is not None
    if with_anchor:
        anchor_ref, stream_ref, inverse_ref = refs[at : at + 3]
        at += 3
        if has_prior:
            sum_ref, square_ref = refs[at : at + 2]
            at += 2
        out_ref, scale_ref = refs[at : at + 2]
        at += 2
    else:
        out_ref = refs[at]
        at += 1
    full, labels, masks, sem = refs[at : at + 4]
    rows = full.shape[1]
    shards = full.shape[0] - 1
    n_slots, _, per_list, tile = tiles_ref.shape[:4]
    group = n_slots * per_list
    per_shard = width // tile
    shift = per_shard.bit_length() - 1

    copies = []
    for i, places in enumerate(plan):
        for at_col, shard, at_row, n_rows in places:
            copies.append(
                pltpu.make_async_copy(
                    src[i].at[:, pl.ds(at_col, width)],
                    full.at[shard, pl.ds(at_row, n_rows)],
                    sem.at[len(copies)],
                )
            )
    for i, at_col, at_row, n_rows in label_plan:
        copies.append(
            pltpu.make_async_copy(
                src[i].at[:, pl.ds(at_col, tile)],
                labels.at[pl.ds(at_row, n_rows)],
                sem.at[len(copies)],
            )
        )
    weights = []
    if with_anchor:
        anchor_buf, anchor_sem = refs[at + 4 : at + 6]
        at_row = 0
        for k, part in enumerate(parts):
            n_rows = len(part) * width
            row = pl.multiple_of(ids_ref[part[0]] * width, width) if len(part) == 1 else 0
            weights.append(
                pltpu.make_async_copy(
                    anchor_ref.at[layer, pl.ds(row, n_rows)],
                    anchor_buf.at[pl.ds(at_row, n_rows)],
                    anchor_sem.at[k],
                )
            )
            at_row += n_rows

    for copy in copies + weights:
        copy.start()
    full[shards, :, 0:tile] = jnp.zeros((rows, tile), BF16)
    for copy in copies:
        copy.wait()
    label = labels[...].astype(F32)
    for t in range(n_slots):
        masks[t] = jnp.where(label == t + 1, 1.0, 0.0).astype(BF16)
    if with_anchor:
        squares = square_ref[...] if has_prior else jnp.zeros((rows, tile), F32)
        for p in range(shards):
            if p not in done:
                squares = square_sum(squares, full.at[p], inverse_ref, p, tile)
        mean = jnp.sum(squares, axis=1, keepdims=True) / (width * shards)
        scale_ref[...] = jnp.broadcast_to(lax.rsqrt(mean + EPS), (rows, tile))
        for copy in weights:
            copy.wait()
        step_cols = col_step * tile
        for n in range(0, width, step_cols):
            lanes = slice(n, n + step_cols)
            anchor_out = jnp.zeros((rows, step_cols), F32)
            for k, p in enumerate([p for part in parts for p in part]):
                anchor_out += jnp.dot(
                    full[p],
                    anchor_buf[k * width : (k + 1) * width, lanes],
                    preferred_element_type=F32,
                )
            if has_prior:
                anchor_out += sum_ref[:, lanes]
            for k in range(0, step_cols, tile):
                out = anchor_out[:, k : k + tile] * scale_ref[...]
                here = slice(n + k, n + k + tile)
                out_ref[:, here] = stream_ref[:, here].astype(F32) + out

    def block_step(step, carry):
        for k in range(col_step):
            c = step * col_step + k
            delta = jnp.zeros((rows, tile), F32)
            for t in range(n_slots):
                pieces = []
                for s in range(per_list):
                    block = ids_ref[shards + c * group + t * per_list + s]
                    shard = lax.shift_right_logical(block, shift)
                    lane = pl.multiple_of(jnp.bitwise_and(block, per_shard - 1) * tile, tile)
                    pieces.append(full[shard, :, pl.ds(lane, tile)] * masks[t])
                delta += jnp.dot(
                    jnp.concatenate(pieces, axis=1),
                    tiles_ref[t, c].reshape(per_list * tile, tile),
                    preferred_element_type=F32,
                )
            cols = pl.ds(pl.multiple_of(c * tile, tile), tile)
            if with_anchor:
                out_ref[:, cols] += (delta * scale_ref[...]).astype(BF16).astype(F32)
            else:
                out_ref[:, cols] = delta.astype(BF16)
        return carry

    lax.fori_loop(0, n_cols // col_step, block_step, 0)


def products(
    ids, sources, plan, label_plan, rows, tiles, layer, col_step,
    parts=None, anchor=None, stream=None, inverse=None, prior=(), done=(),
):
    n_slots, n_cols, per_list, tile, _ = tiles.shape
    shards = 1 + max(place[1] for places in plan for place in places)
    width = n_cols * tile
    with_anchor = parts is not None
    cfg = (
        len(sources), plan, label_plan, parts, bool(prior), done, layer, n_cols, col_step, width,
    )
    in_specs = [in_place()] * len(sources) + [whole()]
    operands = [*sources, tiles]
    out_shape = jax.ShapeDtypeStruct((rows, width), F32 if with_anchor else BF16)
    nbytes = rows * shards * width * 2 + n_slots * n_cols * per_list * tile * tile * 2
    flops = 2 * rows * width * n_slots * per_list * tile
    n_copies = sum(len(places) for places in plan) + len(label_plan)
    scratch = [
        pltpu.VMEM((shards + 1, rows, width), BF16),
        pltpu.VMEM((rows, tile), BF16),
        pltpu.VMEM((n_slots, rows, tile), BF16),
        pltpu.SemaphoreType.DMA((n_copies,)),
    ]
    if with_anchor:
        n_late = sum(len(part) for part in parts)
        in_specs += [in_place()] + [whole()] * (2 + len(prior))
        operands += [anchor, stream, inverse, *prior]
        out_shape = [out_shape, jax.ShapeDtypeStruct((rows, tile), F32)]
        scratch += [
            pltpu.VMEM((n_late * width, width), BF16),
            pltpu.SemaphoreType.DMA((len(parts),)),
        ]
        nbytes += n_late * width * width * 2
        flops += 2 * rows * width * n_late * width
    return pl.pallas_call(
        functools.partial(product_kernel, cfg),
        out_shape=out_shape,
        in_specs=[pl.BlockSpec(memory_space=pltpu.SMEM)] + in_specs,
        out_specs=[whole()] * 2 if with_anchor else whole(),
        scratch_shapes=scratch,
        compiler_params=params(32),
        cost_estimate=pl.CostEstimate(flops=flops, bytes_accessed=nbytes, transcendentals=0),
        name="own_products" if with_anchor else "sent_products",
    )(ids, *operands)


def first_kernel(hidden_ref, gain_ref, y_ref):
    y_ref[...] = (hidden_ref[...].astype(F32) * gain_ref[0:1, :]).astype(BF16)


def first_rows(hidden, norm_gain):
    return pl.pallas_call(
        first_kernel,
        out_shape=jax.ShapeDtypeStruct(hidden.shape, BF16),
        in_specs=[whole()] * 2,
        out_specs=whole(),
        compiler_params=params(8),
        name="first_rows",
    )(hidden, norm_gain)


def join_kernel(n_dest, last, *refs):
    partial_ref, back_ref, scale_ref = refs[:3]
    rets = refs[3 : 3 + n_dest]
    cap = rets[0].shape[0]
    tile = scale_ref.shape[1]
    delta = jnp.zeros(partial_ref.shape, F32)
    for d in range(n_dest):
        delta += jnp.dot(
            back_ref[:, d * cap : (d + 1) * cap], rets[d][...], preferred_element_type=F32
        )
    scale = scale_ref[...]
    for k in range(partial_ref.shape[1] // tile):
        cols = slice(k * tile, (k + 1) * tile)
        routed = (delta[:, cols] * scale).astype(BF16).astype(F32)
        stream = partial_ref[:, cols] + routed
        if last:
            refs[3 + n_dest][:, cols] = stream.astype(BF16)
        else:
            gain_ref, stream_ref, y_ref = refs[3 + n_dest :]
            stream_ref[:, cols] = stream
            y_ref[:, cols] = (stream * gain_ref[:, cols]).astype(BF16)


def join(partial, back, scale, rets, gain):
    rows, width = partial.shape
    last = gain is None
    if last:
        out_shape = jax.ShapeDtypeStruct((rows, width), BF16)
        extra = []
    else:
        out_shape = [
            jax.ShapeDtypeStruct((rows, width), F32),
            jax.ShapeDtypeStruct((rows, width), BF16),
        ]
        extra = [gain]
    return pl.pallas_call(
        functools.partial(join_kernel, len(rets), last),
        out_shape=out_shape,
        in_specs=[whole()] * (3 + len(rets) + len(extra)),
        out_specs=whole() if last else [whole()] * 2,
        compiler_params=params(8),
        cost_estimate=pl.CostEstimate(
            flops=4 * rows * width, bytes_accessed=16 * rows * width, transcendentals=0
        ),
        name="join",
    )(partial, back, scale, *rets, *extra)


def gather_gains(norm_gain, pairwise):
    n_layers, width = norm_gain.shape
    count = lax.axis_size("tp")
    if not pairwise:
        gains = lax.all_gather(norm_gain, "tp", axis=1, tiled=True)
        return gains.reshape(n_layers, count, width)
    gains = norm_gain[:, None, :]
    step = 1
    while step < count:
        gains = jnp.concatenate([gains, swap(gains, "tp", step)], axis=1)
        step *= 2
    return gains


def body(hidden, norm_gain, anchor, delta_tiles, tile_rows, tenant):
    groups = lax.axis_size("group")
    tp_count = lax.axis_size("tp")
    my_group = lax.axis_index("group")
    my_tp = lax.axis_index("tp")
    rows, width = hidden.shape
    per_group, n_layers, _, _, tile, _ = delta_tiles.shape
    row_blocks = width * tp_count // tile
    per_shard = width // tile
    cap = rows // 4
    n_dest = groups - 1
    offsets = list(range(1, groups))
    pairwise = tp_count == 8

    stream = hidden
    y = first_rows(hidden, norm_gain)

    owner = tenant // per_group
    local = tenant % per_group
    dests = jnp.bitwise_xor(my_group, jnp.arange(1, groups, dtype=jnp.int32))
    to_dest = (owner[None, :] == dests[:, None]).astype(jnp.int32)
    rank = jnp.cumsum(to_dest, axis=1) - to_dest
    slot_of = jnp.arange(cap, dtype=jnp.int32)
    hot = (rank[:, None, :] == slot_of[None, :, None]) & (to_dest[:, None, :] > 0)
    hot = hot.reshape(n_dest * cap, rows)
    sel = hot.astype(BF16)
    back = hot.T.astype(BF16)
    label = jnp.broadcast_to((local + 1)[:, None], (rows, tile)).astype(BF16)
    own_label = jnp.where((owner == my_group)[:, None], label, 0.0).astype(BF16)

    base = my_tp if pairwise else jnp.zeros((), jnp.int32)
    blocks = jnp.bitwise_xor(tile_rows, base * per_shard)
    blocks = jnp.where(tile_rows < row_blocks, blocks, row_blocks)
    blocks = blocks.transpose(1, 2, 0, 3).reshape(n_layers, -1)
    shard_of = jnp.bitwise_xor(base, jnp.arange(tp_count, dtype=jnp.int32))
    shard_of = jnp.broadcast_to(shard_of[None, :], (n_layers, tp_count))
    ids_of = jnp.concatenate([shard_of, blocks], axis=1)
    inverse = 1.0 / gather_gains(norm_gain, pairwise)

    if pairwise:
        chunks, early, late = CHUNKS, EARLY, tuple((p,) for p in LATE)
        own_plan = tuple(((0, p, 0, rows),) for p in range(tp_count))
        near_plan = (tuple((p * width, p, 0, cap) for p in range(tp_count)),)
    else:
        chunks = (tuple(range(tp_count)),)
        early, late = (), chunks
        own_plan = (tuple((p * width, p, 0, rows) for p in range(tp_count)),)
        near_plan = (tuple((p * width, p, 0, cap) for p in range(tp_count)),)
    far_plan = tuple(
        tuple((k * width, p, i * cap, cap) for k, p in enumerate(chunk))
        for i in range(1, n_dest)
        for chunk in chunks
    )
    sent_plan = near_plan + far_plan
    n_chunks = len(chunks)
    own_labels = ((len(own_plan), 0, 0, rows),)
    sent_labels = ((0, width * tp_count, 0, cap),) + tuple(
        (1 + (i - 1) * n_chunks, len(chunks[0]) * width, i * cap, cap)
        for i in range(1, n_dest)
    )
    own_plan += ((),)

    for layer in range(n_layers):
        ids = ids_of[layer]
        if pairwise:
            shards = gather_rows(y)
            split = [[shards[p] for p in chunk] for chunk in chunks]
        else:
            shards = [lax.all_gather(y, "tp", axis=1, tiled=True)]
            split = [shards]
        far = [[] for _ in range(n_dest)]
        for q, xs in enumerate(split):
            if q == 0:
                xs = xs + [label]
            picked = pick_rows(sel[cap:], xs, cap)
            for i, d in enumerate(offsets[1:]):
                far[i + 1].append(swap(picked[i], "group", d))
        (picked,) = pick_rows(sel[:cap], shards + [label], cap)
        got = [swap(picked, "group", 1)]
        for pieces in far[1:]:
            got += pieces
        tiles = stage_tiles(delta_tiles, layer)
        prior, done = (), ()
        for part in early:
            row_of = jnp.stack([jnp.bitwise_xor(base, p) for p in part])
            squared = tuple(enumerate(part)) if layer > 0 else ()
            prior = early_products(
                row_of, [shards[p] for p in part], len(part), squared, anchor,
                inverse[layer] if layer > 0 else norm_gain, prior, layer, tile,
            )
            done += tuple(p for _, p in squared)
        partial, scale = products(
            ids, shards + [own_label], own_plan, own_labels, rows, tiles,
            layer, 2,
            parts=late, anchor=anchor, stream=stream, inverse=inverse[layer],
            prior=tuple(prior), done=done,
        )
        answers = products(
            ids, got, sent_plan, sent_labels, n_dest * cap, tiles, layer, 2
        )
        rets = [
            swap(answers[i * cap : (i + 1) * cap], "group", d)
            for i, d in enumerate(offsets)
        ]
        if layer + 1 < n_layers:
            gain = norm_gain[layer + 1][None, :]
            stream, y = join(partial, back, scale, rets, gain)
        else:
            updated = join(partial, back, scale, rets, None)
    return updated


CHUNKS = ((0, 1, 2, 4), (5, 6), (3, 7))
EARLY = ((0, 1), (2, 4), (5, 6))
LATE = (3, 7)


def gather_rows(y):
    near = {0: y}
    near[4] = swap(y, "tp", 4)
    near[2] = swap(y, "tp", 2)
    near[1] = swap(y, "tp", 1)
    near[6] = swap(near[4], "tp", 2)
    near[5] = swap(near[4], "tp", 1)
    near[3] = swap(near[2], "tp", 1)
    near[7] = swap(near[5], "tp", 2)
    return [near[p] for p in range(8)]


def solution(mesh):
    return jax.shard_map(
        body,
        mesh=mesh,
        in_specs=(
            P("group", "tp"),
            P(None, "tp"),
            P(None, None, "tp"),
            P("group", None, "tp", None, None, None),
            P("group", None, "tp", None),
            P("group"),
        ),
        out_specs=P("group", "tp"),
        check_vma=False,
    )
```
